512 devices in a mesh: sample: 8 (over x, z_hi), ctx: 64 (over z_lo, y, core).
Axes of the slice: x: 4, y: 4, z: 16 (z_hi: 2, z_lo: 8; z = z_hi * 8 + z_lo), core: 2. Of those that a mesh axis runs over, the one named last changes fastest.
Arguments:
- queries: bfloat16 [16, 512, 8192], P('sample', None, 'ctx'), may hold values from -8 to 8
- prompt_key_value: bfloat16 [2, 2048, 1024], P(None, 'ctx', 'sample'), may hold values from -6 to 6
- continuation_key_value: bfloat16 [2, 16, 512, 1024], P(None, 'sample', 'ctx'), may hold values from -6 to 6
- page_owner: int32 [2048], replicated, may hold values from 0 to 16, as said below
- cont_lengths: int32 [16], replicated, may hold values from 2 to 512, as said below
- branch_offsets: int32 [16], replicated, may hold values from 512 to 2048
Outputs:
- attended: bfloat16 [16, 512, 8192], P('sample', None, 'ctx')
The draws below stay inside these ranges and needn't reach their ends.
Inputs may be any that keep to these rules, and one draw needn't show every extreme that they name: `page_owner`: constant over each aligned page of 16 positions; 0 marks a page seen by every continuation that branches after it, s + 1 a page seen only by continuation s; some page belongs to continuation 16 - 1. `cont_lengths`: some continuation has all 512 positions live.
All inputs are finite; a program needn't handle non-finite values.
Results may differ from the reference program's by a relative error of at most 0.0045.
Values may be sent and summed in bfloat16 or wider, within the bound.
No kernel may reach another device: no remote copies, remote signals or barrier semaphores. Data moves between devices by JAX's collectives and lax.ppermute only.
A program may use at most 64 MiB of HBM per device.

```python
import jax
import jax.numpy as jnp
from jax import lax

QUERY_HEADS = 64
KEY_VALUE_HEADS = 8
HEAD_SIZE = 128
CONTINUATION_LEN = 512
PAGE = 16
SAMPLE_COUNT = 16
PROMPT_LEN = 2048


def draw_queries(key, part):
    gaussian_portion = jax.random.normal(jax.random.fold_in(key, 11), (SAMPLE_COUNT, CONTINUATION_LEN, QUERY_HEADS * HEAD_SIZE), jnp.float32)
    result = jnp.clip(2.0 * gaussian_portion, -8.0, 8.0)
    return result.astype(jnp.bfloat16)


def draw_continuation_key_value(key, part):
    gaussian_portion = jax.random.normal(jax.random.fold_in(key, 22), (2, SAMPLE_COUNT, CONTINUATION_LEN, KEY_VALUE_HEADS * HEAD_SIZE), jnp.float32)
    result = jnp.clip(gaussian_portion, -6.0, 6.0)
    return result.astype(jnp.bfloat16)


def draw_page_owner(key, part):
    page_count = PROMPT_LEN // PAGE
    shared = jax.random.randint(jax.random.fold_in(key, 44), (page_count,), 0, 2)
    private = jax.random.randint(jax.random.fold_in(key, 45), (page_count,), 1, SAMPLE_COUNT + 1)
    per_page = jnp.where(shared == 0, 0, private)
    chosen = jax.random.randint(jax.random.fold_in(key, 46), (), 0, page_count)
    per_page = jnp.where(jnp.arange(page_count) == chosen, SAMPLE_COUNT, per_page)
    return jnp.repeat(per_page, PAGE).astype(jnp.int32)


def draw_cont_lengths(key, part):
    picked_len = jax.random.randint(jax.random.fold_in(key, 33), (SAMPLE_COUNT,), 2, CONTINUATION_LEN + 1)
    chosen = jax.random.randint(jax.random.fold_in(key, 34), (), 0, SAMPLE_COUNT)
    return jnp.where(jnp.arange(SAMPLE_COUNT) == chosen, CONTINUATION_LEN, picked_len).astype(jnp.int32)


def plant(drawn, stream_key, low, largest):
    index_at = [jax.random.randint(jax.random.fold_in(stream_key, axis), (), 0, length) for axis, length in enumerate(drawn.shape)]
    widest = drawn.shape.index(max(drawn.shape))
    beside = index_at[:widest] + [(index_at[widest] + 1) % drawn.shape[widest]] + index_at[widest + 1:]
    return drawn.at[tuple(index_at)].set(low).at[tuple(beside)].set(largest)


def steps_of(stream_key, extent, pieces, smallest, high):
    def one(position, parts):
        steps = jax.random.uniform(jax.random.fold_in(jax.random.fold_in(stream_key, 6), position), (parts,), jnp.float32, smallest / len(pieces), high / len(pieces))
        return jnp.repeat(jnp.exp(steps), extent[position] // parts).reshape((-1,) + (1,) * (len(extent) - position - 1))

    gain = one(*pieces[0])
    for cut in pieces[1:]:
        gain = gain * one(*cut)
    return gain


def normal_values(key, dims, width, reach, cuts=(), held_as=jnp.bfloat16):
    drawn = width * jax.random.normal(key, dims, jnp.float32)
    if cuts:
        drawn = drawn * steps_of(key, dims, cuts, -0.22, 0.18)
    return jnp.clip(drawn, -reach, reach).astype(held_as)


def setup_inputs(seed: int = 0) -> dict:
    streams_of = jax.random.split(jax.random.key(seed), 7)
    return {
        "queries": draw_queries(jax.random.fold_in(streams_of[6], 71), 0),
        "prompt_key_value": normal_values(streams_of[1], (2, PROMPT_LEN, KEY_VALUE_HEADS * HEAD_SIZE), 1.0, 6.0, ((1, 64), (2, 8))),
        "continuation_key_value": draw_continuation_key_value(jax.random.fold_in(streams_of[6], 71), 0),
        "page_owner": draw_page_owner(jax.random.fold_in(streams_of[6], 71), 0),
        "cont_lengths": draw_cont_lengths(jax.random.fold_in(streams_of[6], 71), 0),
        "branch_offsets": plant(jax.random.randint(streams_of[5], (SAMPLE_COUNT,), PROMPT_LEN // 4, PROMPT_LEN + 1), jax.random.fold_in(streams_of[5], 1), PROMPT_LEN // 4, PROMPT_LEN).astype(jnp.int32),
    }


def reference(queries, prompt_key_value, continuation_key_value, page_owner, cont_lengths, branch_offsets):
    query_groups = QUERY_HEADS // KEY_VALUE_HEADS
    scale = HEAD_SIZE ** -0.5
    query_matrix = queries.reshape(SAMPLE_COUNT, CONTINUATION_LEN, KEY_VALUE_HEADS, query_groups, HEAD_SIZE).transpose(0, 2, 1, 3, 4).reshape(SAMPLE_COUNT * KEY_VALUE_HEADS, CONTINUATION_LEN * query_groups, HEAD_SIZE)
    prompt_key_rows = prompt_key_value[0].reshape(PROMPT_LEN, KEY_VALUE_HEADS, HEAD_SIZE).transpose(1, 0, 2)
    prompt_value_rows = prompt_key_value[1].reshape(PROMPT_LEN, KEY_VALUE_HEADS, HEAD_SIZE).transpose(1, 0, 2)
    continuation_keys = continuation_key_value[0].reshape(SAMPLE_COUNT, CONTINUATION_LEN, KEY_VALUE_HEADS, HEAD_SIZE).transpose(0, 2, 1, 3)
    continuation_values = continuation_key_value[1].reshape(SAMPLE_COUNT, CONTINUATION_LEN, KEY_VALUE_HEADS, HEAD_SIZE).transpose(0, 2, 1, 3)
    prompt_pos = jnp.arange(PROMPT_LEN, dtype=jnp.int32)
    cont_pos = jnp.arange(CONTINUATION_LEN, dtype=jnp.int32)
    row_pos = jnp.arange(CONTINUATION_LEN * query_groups, dtype=jnp.int32) // query_groups

    def single_head(flattened_index):
        sample_number = flattened_index // KEY_VALUE_HEADS
        head_number = flattened_index % KEY_VALUE_HEADS
        rows = query_matrix[flattened_index]
        keys_all = jnp.concatenate([prompt_key_rows[head_number], continuation_keys[sample_number, head_number]], axis=0)
        values_all = jnp.concatenate([prompt_value_rows[head_number], continuation_values[sample_number, head_number]], axis=0)
        scores = jnp.dot(rows, keys_all.T, preferred_element_type=jnp.float32) * scale
        owner_ok = (page_owner == 0) | (page_owner == sample_number + 1)
        prompt_seen = (prompt_pos < branch_offsets[sample_number]) & owner_ok
        length = cont_lengths[sample_number]
        cont_seen = (cont_pos[None, :] <= row_pos[:, None]) & (cont_pos[None, :] < length)
        visible = jnp.concatenate([jnp.broadcast_to(prompt_seen[None, :], (CONTINUATION_LEN * query_groups, PROMPT_LEN)), cont_seen], axis=1)
        masked = jnp.where(visible, scores, -1.0e30)
        row_max = jnp.max(masked, axis=1, keepdims=True)
        weights = jnp.where(visible, jnp.exp(masked - row_max), 0.0)
        weight_sum = jnp.sum(weights, axis=1, keepdims=True)
        mixed = jnp.dot(weights.astype(jnp.bfloat16), values_all, preferred_element_type=jnp.float32) / weight_sum
        return jnp.where((row_pos < length)[:, None], mixed, 0.0)

    output_rows = lax.map(single_head, jnp.arange(SAMPLE_COUNT * KEY_VALUE_HEADS, dtype=jnp.int32))
    output_rows = output_rows.reshape(SAMPLE_COUNT, KEY_VALUE_HEADS, CONTINUATION_LEN, query_groups, HEAD_SIZE).transpose(0, 2, 1, 3, 4)
    return output_rows.reshape(SAMPLE_COUNT, CONTINUATION_LEN, QUERY_HEADS * HEAD_SIZE).astype(jnp.bfloat16)
```

```python
import jax
import jax.numpy as jnp
from jax import lax
from jax.experimental import pallas as pl
from jax.experimental.pallas import tpu as pltpu
from jax.sharding import Mesh, PartitionSpec as P

HEAD_SIZE = 128
KEY_VALUE_HEADS = 8
AXES = ("x", "zh", "zl", "y", "c")
DIMS = (4, 2, 8, 4, 2)
NEG = -1e30
LOG2E = 1.4426950408889634
ROWS = 256


def flat(x, zh, zl, y, c):
    return (((x * 2 + zh) * 8 + zl) * 4 + y) * 2 + c


def block_moves(flip):
    moves = []
    for s in range(8):
        for a in range(8):
            for y in range(4):
                for c in range(2):
                    source = flat(s // 2, s % 2, a, y, c)
                    moves.append((source, flat(a // 2, (a % 2) ^ flip, s, y, c)))
    return moves


def attend(q_ref, own_ref, other_ref, cont_ref, owner_ref, lengths_ref, offsets_ref, out_ref):
    tile = pl.program_id(0)
    per_sample = 512 // ROWS
    here = tile // per_sample
    row0 = (tile % per_sample) * ROWS
    core = lax.axis_index("c")
    flip = lax.axis_index("zh")
    sample = (lax.axis_index("x") * 2 + lax.axis_index("zh")) * 2 + here
    length = lengths_ref[sample]
    offset = offsets_ref[sample]
    q = q_ref[0]
    dims = (((1,), (1,)), ((), ()))
    col = lax.broadcasted_iota(jnp.int32, (1, 1024), 1)
    block = ((col >> 5) & 1) ^ flip
    base = ((2 * (col >> 8) + block) * 4 + ((col >> 6) & 3)) * 64 + (col & 31)
    scores = []
    for ref, which in ((own_ref, core), (other_ref, 1 - core)):
        owner = owner_ref[flip, which].reshape(1, 1024)
        place = base + which * 32
        seen = ((owner == 0) | (owner == sample + 1)) & (place < offset)
        bias = jnp.where(seen, 0.0, NEG)
        keys = ref[:, :, 0].reshape(1024, HEAD_SIZE)
        part = lax.dot_general(q, keys, dims, preferred_element_type=jnp.float32)
        scores.append(part + bias)
    ucol = lax.broadcasted_iota(jnp.int32, (1, 512), 1)
    swap = (ucol >> 8) ^ core
    u = (((ucol >> 3) & 7) * 8 + ((ucol >> 6) & 3) * 2 + swap) * 8 + (ucol & 7)
    t = row0 + lax.broadcasted_iota(jnp.int32, (ROWS, 1), 0)
    part = lax.dot_general(q, cont_ref[0, 0], dims, preferred_element_type=jnp.float32)
    scores.append(jnp.where((u <= t) & (u < length), part, NEG))
    top = scores[0].max(axis=1, keepdims=True)
    for part in scores[1:]:
        top = jnp.maximum(top, part.max(axis=1, keepdims=True))
    total = jnp.zeros((ROWS, 1), jnp.float32)
    mixed = jnp.zeros((ROWS, HEAD_SIZE), jnp.float32)
    values = (
        own_ref[:, :, 1].reshape(1024, HEAD_SIZE),
        other_ref[:, :, 1].reshape(1024, HEAD_SIZE),
        cont_ref[1, 0],
    )
    for part, value in zip(scores, values):
        weights = jnp.exp2((part - top) * (HEAD_SIZE**-0.5 * LOG2E))
        total += weights.sum(axis=1, keepdims=True)
        mixed += jnp.dot(weights.astype(jnp.bfloat16), value, preferred_element_type=jnp.float32)
    out_ref[0] = jnp.where(t < length, mixed / total, 0.0).astype(jnp.bfloat16)


def local(queries, prompt, cont, page_owner, cont_lengths, branch_offsets):
    first = lax.ppermute(prompt, AXES, block_moves(0))
    second = lax.ppermute(prompt, AXES, block_moves(1))
    pieces = cont.reshape(2, 2, 8, KEY_VALUE_HEADS, HEAD_SIZE).transpose(3, 0, 1, 2, 4)
    pieces = lax.all_to_all(pieces, "zl", 0, 0, tiled=True)
    pair = jnp.stack([first, second])
    spread = jnp.broadcast_to(pair[None], (16,) + pair.shape)
    own = lax.all_to_all(spread, ("x", "y"), 0, 0, tiled=True)
    spread = jnp.broadcast_to(pieces[None], (4,) + pieces.shape)
    pieces = lax.all_to_all(spread, "y", 0, 0, tiled=True)
    pieces = pieces.transpose(2, 3, 0, 1, 4, 5).reshape(2, 2, 256, HEAD_SIZE)
    swap = [(0, 1), (1, 0)]
    other = lax.ppermute(own, "c", swap)
    far = lax.ppermute(pieces, "c", swap)
    own_cont = jnp.concatenate([pieces, far], axis=2)
    owner = page_owner.reshape(4, 2, 4, 2, 32).transpose(3, 0, 2, 1, 4)
    owner = jnp.stack([owner, owner[:, :, :, ::-1]]).reshape(2, 2, 8, 128)
    per_sample = 512 // ROWS
    return pl.pallas_call(
        attend,
        grid=(2 * per_sample,),
        out_shape=jax.ShapeDtypeStruct(queries.shape, jnp.bfloat16),
        in_specs=[
            pl.BlockSpec((1, ROWS, HEAD_SIZE), lambda i: (i // per_sample, i % per_sample, 0)),
            pl.BlockSpec((16, 2, 2, 32, HEAD_SIZE), lambda i: (0, 0, 0, 0, 0)),
            pl.BlockSpec((16, 2, 2, 32, HEAD_SIZE), lambda i: (0, 0, 0, 0, 0)),
            pl.BlockSpec((2, 1, 512, HEAD_SIZE), lambda i: (0, i // per_sample, 0, 0)),
            pl.BlockSpec((2, 2, 8, 128), lambda i: (0, 0, 0, 0)),
            pl.BlockSpec(memory_space=pltpu.SMEM),
            pl.BlockSpec(memory_space=pltpu.SMEM),
        ],
        out_specs=pl.BlockSpec(
            (1, ROWS, HEAD_SIZE), lambda i: (i // per_sample, i % per_sample, 0)
        ),
        cost_estimate=pl.CostEstimate(
            flops=1400000000, transcendentals=2700000, bytes_accessed=3000000
        ),
    )(queries, own, other, own_cont, owner, cont_lengths, branch_offsets)


def solution(mesh):
    fine = Mesh(mesh.devices.reshape(DIMS), AXES)
    sample, ctx = ("x", "zh"), ("zl", "y", "c")
    in_specs = (
        P(sample, None, ctx),
        P(None, ctx, sample),
        P(None, sample, ctx, None),
        P(),
        P(),
        P(),
    )
    return jax.shard_map(
        local, mesh=fine, in_specs=in_specs, out_specs=P(sample, None, ctx), check_vma=False
    )
```

```python
import functools
import itertools

import jax
import jax.numpy as jnp
from jax import lax
from jax.experimental import pallas as pl
from jax.experimental.pallas import tpu as pltpu
from jax.sharding import Mesh, PartitionSpec as P


HEAD_SIZE = 128
KEY_VALUE_HEADS = 8
AXES = ("x", "zh", "zl", "y", "c")
DIMS = (4, 2, 8, 4, 2)
NEG = -1e30
FACTOR = HEAD_SIZE**-0.5 * 1.4426950408889634
ROWS = 128
TRANSPOSED = (((1,), (1,)), ((), ()))


def flat(x, zh, zl, y, c):
    return (((x * 2 + zh) * 8 + zl) * 4 + y) * 2 + c


def hops(source, target, size):
    apart = abs(source - target) % size
    return min(apart, size - apart)


def nearest(blocks, head, plane):
    def cost(order):
        lengths = [
            hops(8 * (head % 2) + a, plane, 16) + hops(head // 2, x, 4)
            for a, x in zip(blocks, order)
        ]
        return max(lengths), sum(length * length for length in lengths)

    order = min(itertools.permutations(range(4)), key=cost)
    return cost(order), dict(zip(blocks, order))


def block_plan():
    near, far, slots = {}, {}, []
    for head in range(8):
        best = None
        for low in itertools.combinations(range(8), 4):
            high = tuple(a for a in range(8) if a not in low)
            here = [nearest(low, head, head), nearest(high, head, head + 8)]
            there = [nearest(high, head, head), nearest(low, head, head + 8)]
            cost = (max(h[0] for h in here), max(h[0] for h in there))
            if best is None or cost < best[0]:
                best = (cost, here, there)
        for z in range(2):
            for a, x in best[1][z][1].items():
                near[head, a] = (x, z)
            for a, x in best[2][z][1].items():
                far[head, a] = (x, z)
    for z in range(2):
        for head in range(8):
            packed = 0
            for a in range(8):
                second = near[head, a][1] != z
                x = (far if second else near)[head, a][0]
                packed |= (2 * x + second) << (3 * a)
            slots.append(packed)
    return near, far, slots


NEAR, FAR, SLOTS = block_plan()


def block_moves(plan):
    moves = []
    for (head, a), (x, z) in plan.items():
        for y in range(4):
            for c in range(2):
                moves.append((flat(head // 2, head % 2, a, y, c), flat(x, z, head, y, c)))
    return moves


def first_sample():
    return (lax.axis_index("x") * 2 + lax.axis_index("zh")) * 2


def with_ones(values):
    return jnp.concatenate([values, jnp.ones_like(values)], axis=1)


def weigh(part, top, values):
    wide = jnp.concatenate([top] * (part.shape[1] // HEAD_SIZE), axis=1)
    weights = jnp.exp2((part - wide) * FACTOR).astype(jnp.bfloat16)
    both = jnp.dot(weights, values, preferred_element_type=jnp.float32)
    return both[:, :HEAD_SIZE], both[:, HEAD_SIZE:]


def peak_of(part):
    return jnp.broadcast_to(part.max(axis=1, keepdims=True), (ROWS, HEAD_SIZE))


def split_heads(cont_ref, out_ref):
    for head in range(KEY_VALUE_HEADS):
        piece = cont_ref[:, :, :, head * HEAD_SIZE : (head + 1) * HEAD_SIZE]
        for y in range(4):
            out_ref[head, y] = piece


def repeat_blocks(first_ref, second_ref, out_ref):
    pair = (first_ref[...], second_ref[...])
    for x in range(4):
        for y in range(4):
            for which in range(2):
                out_ref[x, y, which] = pair[which]


TILES = [(here, row) for here in range(2) for row in range(0, 512, ROWS)]


def attend_cont(
    q_ref, near_ref, far_ref, lengths_ref, offsets_ref, owner_ref, top_ref, total_ref, mixed_ref
):
    core = lax.axis_index("c")
    base = first_sample()

    def side(kind, here, row):
        count = (row + ROWS) // 2
        return jnp.concatenate([near_ref[kind, here, :count], far_ref[kind, here, :count]])

    def product(here, row):
        return lax.dot_general(
            q_ref[here, row : row + ROWS],
            side(0, here, row),
            TRANSPOSED,
            preferred_element_type=jnp.float32,
        )

    ahead = product(*TILES[0])
    for index, (here, row) in enumerate(TILES):
        part = ahead
        if index + 1 < len(TILES):
            ahead = product(*TILES[index + 1])
        count = (row + ROWS) // 2
        col = lax.broadcasted_iota(jnp.int32, (1, 2 * count), 1)
        far = col >= count
        col = jnp.where(far, col - count, col)
        u = ((col >> 3) * 2 + jnp.where(far, 1 - core, core)) * 8 + (col & 7)
        t = row + lax.broadcasted_iota(jnp.int32, (ROWS, 1), 0)
        part = jnp.where(u <= jnp.minimum(t, lengths_ref[base + here] - 1), part, NEG)
        top = peak_of(part)
        mixed, total = weigh(part, top, with_ones(side(1, here, row)))
        top_ref[here, row : row + ROWS] = top
        total_ref[here, row : row + ROWS] = total
        mixed_ref[here, row : row + ROWS] = mixed


def attend_prompt(
    last, q_ref, half_ref, owner_ref, lengths_ref, offsets_ref, top_ref, total_ref, mixed_ref, *outs
):
    core = lax.axis_index("c")
    which = 1 - core if last else core
    base = first_sample()
    plane = lax.axis_index("zh") * 8 + lax.axis_index("zl")
    packed = jnp.int32(0)
    for index, slots in enumerate(SLOTS):
        packed = jnp.where(plane == index, jnp.int32(slots), packed)
    keys, values = [], []
    for a in range(8):
        slot = (packed >> (3 * a)) & 7
        keys.append(half_ref[slot >> 1, :, slot & 1, 0].reshape(128, HEAD_SIZE))
        values.append(half_ref[slot >> 1, :, slot & 1, 1].reshape(128, HEAD_SIZE))
    keys = jnp.concatenate(keys)
    values = with_ones(jnp.concatenate(values))
    col = lax.broadcasted_iota(jnp.int32, (1, 1024), 1)
    place = (col >> 5) * 64 + which * 32 + (col & 31)
    owner = owner_ref[which].reshape(1, 1024)
    biases = []
    for here in range(2):
        seen = (owner == 0) | (owner == base + here + 1)
        biases.append(jnp.where(seen & (place < offsets_ref[base + here]), 0.0, NEG))

    def product(here, row):
        return lax.dot_general(
            q_ref[here, row : row + ROWS], keys, TRANSPOSED, preferred_element_type=jnp.float32
        )

    ahead = product(*TILES[0])
    for index, (here, row) in enumerate(TILES):
        part = ahead
        if index + 1 < len(TILES):
            ahead = product(*TILES[index + 1])
        rows = slice(row, row + ROWS)
        part = part + biases[here]
        before = top_ref[here, rows]
        top = jnp.maximum(before, peak_of(part))
        mixed, total = weigh(part, top, values)
        shrink = jnp.exp2((before - top) * FACTOR)
        mixed += mixed_ref[here, rows] * shrink
        total += total_ref[here, rows] * shrink
        if last:
            t = row + lax.broadcasted_iota(jnp.int32, (ROWS, 1), 0)
            mixed = jnp.where(t < lengths_ref[base + here], mixed / total, 0.0)
            outs[0][here, rows] = mixed.astype(jnp.bfloat16)
        else:
            outs[0][here, rows] = top
            outs[1][here, rows] = total
            outs[2][here, rows] = mixed


def call(kernel, out_shape, flops, *operands):
    vmem = pl.BlockSpec(memory_space=pltpu.VMEM)
    smem = pl.BlockSpec(memory_space=pltpu.SMEM)
    return pl.pallas_call(
        kernel,
        out_shape=out_shape,
        in_specs=[smem if operand.ndim == 1 else vmem for operand in operands],
        out_specs=jax.tree.map(lambda _: vmem, out_shape),
        compiler_params=pltpu.CompilerParams(vmem_limit_bytes=24 << 20),
        cost_estimate=pl.CostEstimate(
            flops=flops, transcendentals=flops // 512, bytes_accessed=2000000
        ),
    )(*operands)


def local(queries, prompt, cont, page_owner, cont_lengths, branch_offsets):
    owner = page_owner.reshape(32, 2, 32).transpose(1, 0, 2).reshape(2, 8, 128)
    pieces = call(
        split_heads, jax.ShapeDtypeStruct((8, 4, 2, 2, 8, HEAD_SIZE), cont.dtype), 0, cont
    ).reshape(32, 2, 2, 8, HEAD_SIZE)
    near = lax.all_to_all(pieces, ("zl", "y"), 0, 0, tiled=True)
    first = lax.ppermute(prompt, AXES, block_moves(NEAR))
    second = lax.ppermute(prompt, AXES, block_moves(FAR))
    spread = call(
        repeat_blocks,
        jax.ShapeDtypeStruct((4, 4, 2) + first.shape, first.dtype),
        0,
        first,
        second,
    )
    own = lax.all_to_all(
        spread.reshape((16, 2) + first.shape), ("x", "y"), 0, 0, tiled=True
    ).reshape(spread.shape)
    near = near.transpose(1, 2, 0, 3, 4).reshape(2, 2, 256, HEAD_SIZE)
    swap = [(0, 1), (1, 0)]
    far = lax.ppermute(near, "c", swap)
    wide = jax.ShapeDtypeStruct(queries.shape, jnp.float32)
    state = call(
        attend_cont,
        (wide, wide, wide),
        200000000,
        queries,
        near,
        far,
        cont_lengths,
        branch_offsets,
        owner,
    )
    other = lax.ppermute(own, "c", swap)
    state = call(
        functools.partial(attend_prompt, False),
        (wide, wide, wide),
        550000000,
        queries,
        own,
        owner,
        cont_lengths,
        branch_offsets,
        *state,
    )
    return call(
        functools.partial(attend_prompt, True),
        jax.ShapeDtypeStruct(queries.shape, jnp.bfloat16),
        550000000,
        queries,
        other,
        owner,
        cont_lengths,
        branch_offsets,
        *state,
    )


def solution(mesh):
    fine = Mesh(mesh.devices.reshape(DIMS), AXES)
    sample, ctx = ("x", "zh"), ("zl", "y", "c")
    in_specs = (
        P(sample, None, ctx),
        P(None, ctx, sample),
        P(None, sample, ctx, None),
        P(),
        P(),
        P(),
    )
    return jax.shard_map(
        local, mesh=fine, in_specs=in_specs, out_specs=P(sample, None, ctx), check_vma=False
    )
```

```python
import jax
import jax.numpy as jnp
from jax import lax
from jax.experimental import pallas as pl
from jax.experimental.pallas import tpu as pltpu
from jax.sharding import Mesh, PartitionSpec as P


HEAD_SIZE = 128
KEY_VALUE_HEADS = 8
AXES = ("x", "zh", "zl", "y", "c")
DIMS = (4, 2, 8, 4, 2)
NEG = -1e30
FACTOR = HEAD_SIZE**-0.5 * 1.4426950408889634
ROWS = 128
TRANSPOSED = (((1,), (1,)), ((), ()))


def flat(x, zh, zl, y, c):
    return (((x * 2 + zh) * 8 + zl) * 4 + y) * 2 + c


def hops(source, target, size):
    apart = abs(source - target) % size
    return min(apart, size - apart)


def block_plan():
    plan, chunks = {}, []
    for z in range(2):
        for head in range(8):
            places = [(x, c) for x in range(4) for c in range(2)]
            places.sort(key=lambda place: hops(head // 2, place[0], 4))
            blocks = sorted(range(8), key=lambda a: -hops(8 * (head % 2) + a, head + 8 * z, 16))
            packed = 0
            for a, (x, c) in zip(blocks, places):
                plan[z, head, a] = (x, c)
                packed |= a << (12 * c + 3 * x)
            chunks.append(packed)
    return plan, chunks


PLAN, CHUNKS = block_plan()


def block_moves():
    moves = []
    for (z, head, a), (x, c) in PLAN.items():
        for y in range(4):
            moves.append((flat(head // 2, head % 2, a, y, z), flat(x, z, head, y, c)))
    return moves


def first_sample():
    return (lax.axis_index("x") * 2 + lax.axis_index("zh")) * 2


def with_ones(values):
    return jnp.concatenate([values, jnp.ones_like(values)], axis=1)


def weigh(part, top, values):
    wide = jnp.concatenate([top] * (part.shape[1] // HEAD_SIZE), axis=1)
    weights = jnp.exp2((part - wide) * FACTOR).astype(jnp.bfloat16)
    both = jnp.dot(weights, values, preferred_element_type=jnp.float32)
    return both[:, :HEAD_SIZE], both[:, HEAD_SIZE:]


def peak_of(part):
    return jnp.broadcast_to(part.max(axis=1, keepdims=True), (ROWS, HEAD_SIZE))


def split_heads(cont_ref, out_ref):
    for head in range(KEY_VALUE_HEADS):
        piece = cont_ref[:, :, :, head * HEAD_SIZE : (head + 1) * HEAD_SIZE]
        for core in range(2):
            out_ref[head, core] = piece


def repeat_blocks(pair_ref, out_ref):
    pair = pair_ref[...]
    for x in range(4):
        for y in range(4):
            out_ref[x, y] = pair


TILES = [(here, row) for here in range(2) for row in range(0, 512, ROWS)]


def prompt_half(half_ref):
    keys = half_ref[:, :, :, 0].reshape(1024, HEAD_SIZE)
    return keys, with_ones(half_ref[:, :, :, 1].reshape(1024, HEAD_SIZE))


def prompt_biases(which, owner_ref, offsets_ref):
    base = first_sample()
    plane = lax.axis_index("zh") * 8 + lax.axis_index("zl")
    packed = jnp.int32(0)
    for index, chunks in enumerate(CHUNKS):
        packed = jnp.where(plane == index, jnp.int32(chunks), packed)
    col = lax.broadcasted_iota(jnp.int32, (1, 256), 1)
    owners, places = [], []
    for x in range(4):
        chunk = (packed >> (12 * which + 3 * x)) & 7
        owner = owner_ref[chunk]
        owners += [owner[0:1], owner[1:2]]
        places.append(chunk * 256 + col)
    owner = jnp.concatenate(owners, axis=1)
    place = jnp.concatenate(places, axis=1)
    biases = []
    for here in range(2):
        seen = (owner == 0) | (owner == base + here + 1)
        biases.append(jnp.where(seen & (place < offsets_ref[base + here]), 0.0, NEG))
    return biases


def scores(q, keys):
    return lax.dot_general(q, keys, TRANSPOSED, preferred_element_type=jnp.float32)


def attend_own(
    q_ref, half_ref, owner_ref, lengths_ref, offsets_ref, top_ref, total_ref, mixed_ref
):
    keys, values = prompt_half(half_ref)
    biases = prompt_biases(lax.axis_index("c"), owner_ref, offsets_ref)

    def product(here, row):
        return scores(q_ref[here, row : row + ROWS], keys)

    ahead = product(*TILES[0])
    for index, (here, row) in enumerate(TILES):
        part = ahead
        if index + 1 < len(TILES):
            ahead = product(*TILES[index + 1])
        rows = slice(row, row + ROWS)
        part = part + biases[here]
        top = peak_of(part)
        mixed, total = weigh(part, top, values)
        top_ref[here, rows] = top
        total_ref[here, rows] = total
        mixed_ref[here, rows] = mixed


def attend_rest(
    q_ref,
    half_ref,
    near_ref,
    far_ref,
    owner_ref,
    lengths_ref,
    offsets_ref,
    top_ref,
    total_ref,
    mixed_ref,
    out_ref,
):
    base = first_sample()
    keys, values = prompt_half(half_ref)
    biases = prompt_biases(1 - lax.axis_index("c"), owner_ref, offsets_ref)

    def side(kind, here, row):
        count = (row + ROWS) // 4
        return jnp.concatenate(
            [ref[kind, here, k, :count] for ref in (near_ref, far_ref) for k in range(2)]
        )

    def product(here, row):
        q = q_ref[here, row : row + ROWS]
        return scores(q, keys), scores(q, side(0, here, row))

    ahead = product(*TILES[0])
    for index, (here, row) in enumerate(TILES):
        part, cont = ahead
        if index + 1 < len(TILES):
            ahead = product(*TILES[index + 1])
        rows = slice(row, row + ROWS)
        part = part + biases[here]
        count = (row + ROWS) // 4
        col = lax.broadcasted_iota(jnp.int32, (1, 4 * count), 1)
        step = (col >= count).astype(jnp.int32)
        step += (col >= 2 * count).astype(jnp.int32) + (col >= 3 * count).astype(jnp.int32)
        col = col - step * count
        y = lax.axis_index("y") ^ step ^ (step >> 1)
        u = (col >> 4) * 64 + y * 16 + (col & 15)
        t = row + lax.broadcasted_iota(jnp.int32, (ROWS, 1), 0)
        length = lengths_ref[base + here]
        cont = jnp.where(u <= jnp.minimum(t, length - 1), cont, NEG)
        before = top_ref[here, rows]
        top = jnp.maximum(before, jnp.maximum(peak_of(part), peak_of(cont)))
        mixed, total = weigh(part, top, values)
        more = weigh(cont, top, with_ones(side(1, here, row)))
        shrink = jnp.exp2((before - top) * FACTOR)
        mixed += more[0] + mixed_ref[here, rows] * shrink
        total += more[1] + total_ref[here, rows] * shrink
        out_ref[here, rows] = jnp.where(t < length, mixed / total, 0.0).astype(jnp.bfloat16)


def call(kernel, out_shape, flops, *operands):
    vmem = pl.BlockSpec(memory_space=pltpu.VMEM)
    smem = pl.BlockSpec(memory_space=pltpu.SMEM)
    return pl.pallas_call(
        kernel,
        out_shape=out_shape,
        in_specs=[smem if operand.ndim == 1 else vmem for operand in operands],
        out_specs=jax.tree.map(lambda _: vmem, out_shape),
        compiler_params=pltpu.CompilerParams(vmem_limit_bytes=24 << 20),
        cost_estimate=pl.CostEstimate(
            flops=flops, transcendentals=flops // 512, bytes_accessed=2000000
        ),
    )(*operands)


def local(queries, prompt, cont, page_owner, cont_lengths, branch_offsets):
    owner = page_owner.reshape(8, 2, 128)
    pieces = call(
        split_heads, jax.ShapeDtypeStruct((8, 2, 2, 2, 8, HEAD_SIZE), cont.dtype), 0, cont
    ).reshape(16, 2, 2, 8, HEAD_SIZE)
    mine = lax.all_to_all(pieces, ("zl", "c"), 0, 0, tiled=True)
    pair = lax.all_gather(prompt, "c")
    pair = lax.ppermute(pair, AXES, block_moves())
    spread = call(repeat_blocks, jax.ShapeDtypeStruct((4, 4) + pair.shape, pair.dtype), 0, pair)
    own = lax.all_to_all(
        spread.reshape((16,) + pair.shape), ("x", "y"), 0, 0, tiled=True
    ).reshape(spread.shape)
    beside = lax.ppermute(mine, "y", [(0, 1), (1, 0), (2, 3), (3, 2)])
    near = jnp.stack([mine, beside]).transpose(2, 3, 0, 1, 4, 5)
    near = near.reshape(2, 2, 2, 128, HEAD_SIZE)
    far = lax.ppermute(near, "y", [(0, 3), (3, 0), (1, 2), (2, 1)])
    other = lax.ppermute(own, "c", [(0, 1), (1, 0)])
    wide = jax.ShapeDtypeStruct(queries.shape, jnp.float32)
    state = call(
        attend_own,
        (wide, wide, wide),
        550000000,
        queries,
        own,
        owner,
        cont_lengths,
        branch_offsets,
    )
    return call(
        attend_rest,
        jax.ShapeDtypeStruct(queries.shape, jnp.bfloat16),
        750000000,
        queries,
        other,
        near,
        far,
        owner,
        cont_lengths,
        branch_offsets,
        *state,
    )


def solution(mesh):
    fine = Mesh(mesh.devices.reshape(DIMS), AXES)
    sample, ctx = ("x", "zh"), ("zl", "y", "c")
    in_specs = (
        P(sample, None, ctx),
        P(None, ctx, sample),
        P(None, sample, ctx, None),
        P(),
        P(),
        P(),
    )
    return jax.shard_map(
        local, mesh=fine, in_specs=in_specs, out_specs=P(sample, None, ctx), check_vma=False
    )
```

```python
import jax
import jax.numpy as jnp
from jax import lax
from jax.experimental import pallas as pl
from jax.experimental.pallas import tpu as pltpu
from jax.sharding import Mesh, PartitionSpec as P


HEAD_SIZE = 128
KEY_VALUE_HEADS = 8
AXES = ("x", "zh", "zl", "y", "c")
DIMS = (4, 2, 8, 4, 2)
NEG = -1e30
FACTOR = HEAD_SIZE**-0.5 * 1.4426950408889634
ROWS = 128
TRANSPOSED = (((1,), (1,)), ((), ()))


def flat(x, zh, zl, y, c):
    return (((x * 2 + zh) * 8 + zl) * 4 + y) * 2 + c


def hops(source, target, size):
    apart = abs(source - target) % size
    return min(apart, size - apart)


def block_plan():
    plan, chunks = {}, []
    for z in range(2):
        for head in range(8):
            places = [(x, c) for x in range(4) for c in range(2)]
            places.sort(key=lambda place: hops(head // 2, place[0], 4))
            blocks = sorted(range(8), key=lambda a: -hops(8 * (head % 2) + a, head + 8 * z, 16))
            packed = 0
            for a, (x, c) in zip(blocks, places):
                plan[z, head, a] = (x, c)
                packed |= a << (12 * c + 3 * x)
            chunks.append(packed)
    return plan, chunks


PLAN, CHUNKS = block_plan()


def block_moves():
    moves = []
    for (z, head, a), (x, c) in PLAN.items():
        for y in range(4):
            moves.append((flat(head // 2, head % 2, a, y, z), flat(x, z, head, y, c)))
    return moves


def first_sample():
    return (lax.axis_index("x") * 2 + lax.axis_index("zh")) * 2


def with_ones(values):
    return jnp.concatenate([values, jnp.ones_like(values)], axis=1)


def weigh(part, top, values):
    wide = jnp.concatenate([top] * (part.shape[1] // HEAD_SIZE), axis=1)
    weights = jnp.exp2((part - wide) * FACTOR).astype(jnp.bfloat16)
    both = jnp.dot(weights, values, preferred_element_type=jnp.float32)
    return both[:, :HEAD_SIZE], both[:, HEAD_SIZE:]


def peak_of(part):
    return jnp.broadcast_to(part.max(axis=1, keepdims=True), (ROWS, HEAD_SIZE))


def split_heads(cont_ref, out_ref):
    for head in range(KEY_VALUE_HEADS):
        piece = cont_ref[:, :, :, head * HEAD_SIZE : (head + 1) * HEAD_SIZE]
        for core in range(2):
            out_ref[head, core] = piece


def repeat_blocks(pair_ref, out_ref):
    pair = pair_ref[...]
    for x in range(4):
        for y in range(4):
            out_ref[x, y] = pair


def run_tiles(tiles, product, consume):
    ahead = product(*tiles[0])
    for index, tile in enumerate(tiles):
        part = ahead
        if index + 1 < len(tiles):
            ahead = product(*tiles[index + 1])
        consume(*tile, part)


def live_rows(lengths_ref, product, consume, blank=None):
    base = first_sample()
    run_tiles([(here, row) for here in range(2) for row in (0, ROWS)], product, consume)
    for here in range(2):
        length = lengths_ref[base + here]
        tiles = [(here, 2 * ROWS), (here, 3 * ROWS)]

        @pl.when(length > 3 * ROWS)
        def _():
            run_tiles(tiles, product, consume)

        @pl.when((length > 2 * ROWS) & (length <= 3 * ROWS))
        def _():
            run_tiles(tiles[:1], product, consume)
            if blank is not None:
                blank(*tiles[1])

        if blank is not None:

            @pl.when(length <= 2 * ROWS)
            def _():
                for tile in tiles:
                    blank(*tile)


def prompt_side(half_ref, kind):
    return half_ref[:, :, :, kind].reshape(1024, HEAD_SIZE)


def prompt_biases(which, owner_ref, offsets_ref):
    base = first_sample()
    plane = lax.axis_index("zh") * 8 + lax.axis_index("zl")
    packed = jnp.int32(0)
    for index, chunks in enumerate(CHUNKS):
        packed = jnp.where(plane == index, jnp.int32(chunks), packed)
    col = lax.broadcasted_iota(jnp.int32, (1, 256), 1)
    owners, places = [], []
    for x in range(4):
        chunk = (packed >> (12 * which + 3 * x)) & 7
        owner = owner_ref[chunk]
        owners += [owner[0:1], owner[1:2]]
        places.append(chunk * 256 + col)
    owner = jnp.concatenate(owners, axis=1)
    place = jnp.concatenate(places, axis=1)
    biases = []
    for here in range(2):
        seen = (owner == 0) | (owner == base + here + 1)
        biases.append(jnp.where(seen & (place < offsets_ref[base + here]), 0.0, NEG))
    return biases


def scores(q, keys):
    return lax.dot_general(q, keys, TRANSPOSED, preferred_element_type=jnp.float32)


def cont_side(ref, kind, here, row):
    count = 64 if row < 2 * ROWS else 128
    return jnp.concatenate([ref[kind, here, 0, :count], ref[kind, here, 1, :count]])


def cont_mask(cont, far, row, length):
    count = cont.shape[1] // 2
    col = lax.broadcasted_iota(jnp.int32, (1, 2 * count), 1)
    step = (col >= count).astype(jnp.int32)
    col = col - step * count
    y = lax.axis_index("y") ^ step ^ (3 if far else 0)
    u = (col >> 4) * 64 + y * 16 + (col & 15)
    t = row + lax.broadcasted_iota(jnp.int32, (ROWS, 1), 0)
    return jnp.where(u <= jnp.minimum(t, length - 1), cont, NEG)


def attend_near(
    q_ref, near_ref, lengths_ref, offsets_ref, owner_ref, top_ref, total_ref, mixed_ref
):
    base = first_sample()

    def product(here, row):
        return scores(q_ref[here, row : row + ROWS], cont_side(near_ref, 0, here, row))

    def consume(here, row, cont):
        cont = cont_mask(cont, False, row, lengths_ref[base + here])
        top = peak_of(cont)
        mixed, total = weigh(cont, top, with_ones(cont_side(near_ref, 1, here, row)))
        top_ref[here, row : row + ROWS] = top
        total_ref[here, row : row + ROWS] = total
        mixed_ref[here, row : row + ROWS] = mixed

    live_rows(lengths_ref, product, consume)


def attend_own(
    q_ref,
    half_ref,
    owner_ref,
    lengths_ref,
    offsets_ref,
    top_ref,
    total_ref,
    mixed_ref,
    top_out,
    total_out,
    mixed_out,
):
    biases = prompt_biases(lax.axis_index("c"), owner_ref, offsets_ref)

    def product(here, row):
        return scores(q_ref[here, row : row + ROWS], prompt_side(half_ref, 0))

    def consume(here, row, part):
        rows = slice(row, row + ROWS)
        part = part + biases[here]
        before = top_ref[here, rows]
        top = jnp.maximum(before, peak_of(part))
        mixed, total = weigh(part, top, with_ones(prompt_side(half_ref, 1)))
        shrink = jnp.exp2((before - top) * FACTOR)
        top_out[here, rows] = top
        total_out[here, rows] = total + total_ref[here, rows] * shrink
        mixed_out[here, rows] = mixed + mixed_ref[here, rows] * shrink

    live_rows(lengths_ref, product, consume)


def attend_rest(
    q_ref,
    half_ref,
    far_ref,
    owner_ref,
    lengths_ref,
    offsets_ref,
    top_ref,
    total_ref,
    mixed_ref,
    out_ref,
):
    base = first_sample()
    biases = prompt_biases(1 - lax.axis_index("c"), owner_ref, offsets_ref)

    def product(here, row):
        q = q_ref[here, row : row + ROWS]
        return scores(q, prompt_side(half_ref, 0)), scores(q, cont_side(far_ref, 0, here, row))

    def consume(here, row, parts):
        rows = slice(row, row + ROWS)
        length = lengths_ref[base + here]
        part = parts[0] + biases[here]
        cont = cont_mask(parts[1], True, row, length)
        before = top_ref[here, rows]
        top = jnp.maximum(before, jnp.maximum(peak_of(part), peak_of(cont)))
        mixed, total = weigh(part, top, with_ones(prompt_side(half_ref, 1)))
        more = weigh(cont, top, with_ones(cont_side(far_ref, 1, here, row)))
        shrink = jnp.exp2((before - top) * FACTOR)
        mixed += more[0] + mixed_ref[here, rows] * shrink
        total += more[1] + total_ref[here, rows] * shrink
        t = row + lax.broadcasted_iota(jnp.int32, (ROWS, 1), 0)
        out_ref[here, rows] = jnp.where(t < length, mixed / total, 0.0).astype(jnp.bfloat16)

    def blank(here, row):
        out_ref[here, row : row + ROWS] = jnp.zeros((ROWS, HEAD_SIZE), jnp.bfloat16)

    live_rows(lengths_ref, product, consume, blank)


def call(kernel, out_shape, flops, *operands):
    vmem = pl.BlockSpec(memory_space=pltpu.VMEM)
    smem = pl.BlockSpec(memory_space=pltpu.SMEM)
    return pl.pallas_call(
        kernel,
        out_shape=out_shape,
        in_specs=[smem if operand.ndim == 1 else vmem for operand in operands],
        out_specs=jax.tree.map(lambda _: vmem, out_shape),
        compiler_params=pltpu.CompilerParams(vmem_limit_bytes=24 << 20),
        cost_estimate=pl.CostEstimate(
            flops=flops, transcendentals=flops // 512, bytes_accessed=2000000
        ),
    )(*operands)


def local(queries, prompt, cont, page_owner, cont_lengths, branch_offsets):
    owner = page_owner.reshape(8, 2, 128)
    pieces = call(
        split_heads, jax.ShapeDtypeStruct((8, 2, 2, 2, 8, HEAD_SIZE), cont.dtype), 0, cont
    ).reshape(16, 2, 2, 8, HEAD_SIZE)
    mine = lax.all_to_all(pieces, ("zl", "c"), 0, 0, tiled=True)
    pair = lax.all_gather(prompt, "c")
    pair = lax.ppermute(pair, AXES, block_moves())
    spread = call(
        repeat_blocks, jax.ShapeDtypeStruct((4, 4) + pair.shape, pair.dtype), 0, pair
    )
    own = lax.all_to_all(
        spread.reshape((16,) + pair.shape), ("x", "y"), 0, 0, tiled=True
    ).reshape(spread.shape)
    beside = lax.ppermute(mine, "y", [(0, 1), (1, 0), (2, 3), (3, 2)])
    near = jnp.stack([mine, beside]).transpose(2, 3, 0, 1, 4, 5)
    near = near.reshape(2, 2, 2, 128, HEAD_SIZE)
    far = lax.ppermute(near, "y", [(0, 3), (3, 0), (1, 2), (2, 1)])
    other = lax.ppermute(own, "c", [(0, 1), (1, 0)])
    wide = jax.ShapeDtypeStruct(queries.shape, jnp.float32)
    state = call(
        attend_near,
        (wide, wide, wide),
        100000000,
        queries,
        near,
        cont_lengths,
        branch_offsets,
        owner,
    )
    state = call(
        attend_own,
        (wide, wide, wide),
        550000000,
        queries,
        own,
        owner,
        cont_lengths,
        branch_offsets,
        *state,
    )
    return call(
        attend_rest,
        jax.ShapeDtypeStruct(queries.shape, jnp.bfloat16),
        650000000,
        queries,
        other,
        far,
        owner,
        cont_lengths,
        branch_offsets,
        *state,
    )


def solution(mesh):
    fine = Mesh(mesh.devices.reshape(DIMS), AXES)
    sample, ctx = ("x", "zh"), ("zl", "y", "c")
    in_specs = (
        P(sample, None, ctx),
        P(None, ctx, sample),
        P(None, sample, ctx, None),
        P(),
        P(),
        P(),
    )
    return jax.shard_map(
        local, mesh=fine, in_specs=in_specs, out_specs=P(sample, None, ctx), check_vma=False
    )
```

```python
import jax
import jax.numpy as jnp
from jax import lax
from jax.experimental import pallas as pl
from jax.experimental.pallas import tpu as pltpu
from jax.sharding import Mesh, PartitionSpec as P


HEAD_SIZE = 128
KEY_VALUE_HEADS = 8
AXES = ("x", "zh", "zl", "y", "c")
DIMS = (4, 2, 8, 4, 2)
NEG = -1e30
FACTOR = HEAD_SIZE**-0.5 * 1.4426950408889634
ROWS = 128
TRANSPOSED = (((1,), (1,)), ((), ()))


def flat(x, zh, zl, y, c):
    return (((x * 2 + zh) * 8 + zl) * 4 + y) * 2 + c


def hops(source, target, size):
    apart = abs(source - target) % size
    return min(apart, size - apart)


def block_plan():
    plan, chunks = {}, []
    for z in range(2):
        for head in range(8):
            places = [(x, c) for x in range(4) for c in range(2)]
            places.sort(key=lambda place: hops(head // 2, place[0], 4))
            blocks = sorted(range(8), key=lambda a: -hops(8 * (head % 2) + a, head + 8 * z, 16))
            packed = 0
            for a, (x, c) in zip(blocks, places):
                plan[z, head, a] = (x, c)
                packed |= a << (12 * c + 3 * x)
            chunks.append(packed)
    return plan, chunks


PLAN, CHUNKS = block_plan()


def block_moves():
    moves = []
    for (z, head, a), (x, c) in PLAN.items():
        for y in range(4):
            moves.append((flat(head // 2, head % 2, a, y, z), flat(x, z, head, y, c)))
    return moves


def first_sample():
    return (lax.axis_index("x") * 2 + lax.axis_index("zh")) * 2


def with_ones(values):
    return jnp.concatenate([values, jnp.ones_like(values)], axis=1)


def weigh(part, top, values):
    wide = jnp.concatenate([top] * (part.shape[1] // HEAD_SIZE), axis=1)
    weights = jnp.exp2((part - wide) * FACTOR).astype(jnp.bfloat16)
    both = jnp.dot(weights, values, preferred_element_type=jnp.float32)
    return both[:, :HEAD_SIZE], both[:, HEAD_SIZE:]


def peak_of(part):
    return jnp.broadcast_to(part.max(axis=1, keepdims=True), (ROWS, HEAD_SIZE))


def split_heads(cont_ref, out_ref):
    for head in range(KEY_VALUE_HEADS):
        piece = cont_ref[:, :, :, head * HEAD_SIZE : (head + 1) * HEAD_SIZE]
        for core in range(2):
            out_ref[head, core] = piece


def repeat_blocks(pair_ref, out_ref):
    pair = pair_ref[...]
    for x in range(4):
        for y in range(4):
            out_ref[x, y] = pair


def run_tiles(tiles, product, consume):
    ahead = product(*tiles[0])
    for index, tile in enumerate(tiles):
        part = ahead
        if index + 1 < len(tiles):
            ahead = product(*tiles[index + 1])
        consume(*tile, part)


def live_rows(lengths_ref, product, consume, blank=None):
    base = first_sample()
    run_tiles([(here, row) for here in range(2) for row in (0, ROWS)], product, consume)
    for here in range(2):
        length = lengths_ref[base + here]
        tiles = [(here, 2 * ROWS), (here, 3 * ROWS)]

        @pl.when(length > 3 * ROWS)
        def _():
            run_tiles(tiles, product, consume)

        @pl.when((length > 2 * ROWS) & (length <= 3 * ROWS))
        def _():
            run_tiles(tiles[:1], product, consume)
            if blank is not None:
                blank(*tiles[1])

        if blank is not None:

            @pl.when(length <= 2 * ROWS)
            def _():
                for tile in tiles:
                    blank(*tile)


def prompt_side(half_ref, kind):
    return half_ref[:, :, :, kind].reshape(1024, HEAD_SIZE)


def prompt_biases(which, owner_ref, offsets_ref):
    base = first_sample()
    plane = lax.axis_index("zh") * 8 + lax.axis_index("zl")
    packed = jnp.int32(0)
    for index, chunks in enumerate(CHUNKS):
        packed = jnp.where(plane == index, jnp.int32(chunks), packed)
    col = lax.broadcasted_iota(jnp.int32, (1, 256), 1)
    owners, places = [], []
    for x in range(4):
        chunk = (packed >> (12 * which + 3 * x)) & 7
        owner = owner_ref[chunk]
        owners += [owner[0:1], owner[1:2]]
        places.append(chunk * 256 + col)
    owner = jnp.concatenate(owners, axis=1)
    place = jnp.concatenate(places, axis=1)
    biases = []
    for here in range(2):
        seen = (owner == 0) | (owner == base + here + 1)
        biases.append(jnp.where(seen & (place < offsets_ref[base + here]), 0.0, NEG))
    return biases


def scores(q, keys):
    return lax.dot_general(q, keys, TRANSPOSED, preferred_element_type=jnp.float32)


def cont_side(ref, kind, here, row):
    count = 64 if row < 2 * ROWS else 128
    return jnp.concatenate([ref[kind, here, 0, :count], ref[kind, here, 1, :count]])


def cont_mask(cont, far, row, length):
    count = cont.shape[1] // 2
    col = lax.broadcasted_iota(jnp.int32, (1, 2 * count), 1)
    step = (col >= count).astype(jnp.int32)
    col = col - step * count
    y = lax.axis_index("y") ^ (3 * step) ^ (1 if far else 0)
    u = (col >> 4) * 64 + y * 16 + (col & 15)
    t = row + lax.broadcasted_iota(jnp.int32, (ROWS, 1), 0)
    return jnp.where(u <= jnp.minimum(t, length - 1), cont, NEG)


def attend_near(
    q_ref, near_ref, lengths_ref, offsets_ref, owner_ref, top_ref, total_ref, mixed_ref
):
    base = first_sample()

    def product(here, row):
        return scores(q_ref[here, row : row + ROWS], cont_side(near_ref, 0, here, row))

    def consume(here, row, cont):
        cont = cont_mask(cont, False, row, lengths_ref[base + here])
        top = peak_of(cont)
        mixed, total = weigh(cont, top, with_ones(cont_side(near_ref, 1, here, row)))
        top_ref[here, row : row + ROWS] = top
        total_ref[here, row : row + ROWS] = total
        mixed_ref[here, row : row + ROWS] = mixed

    live_rows(lengths_ref, product, consume)


def attend_own(
    q_ref,
    half_ref,
    owner_ref,
    lengths_ref,
    offsets_ref,
    top_ref,
    total_ref,
    mixed_ref,
    top_out,
    total_out,
    mixed_out,
):
    biases = prompt_biases(lax.axis_index("c"), owner_ref, offsets_ref)

    def product(here, row):
        return scores(q_ref[here, row : row + ROWS], prompt_side(half_ref, 0))

    def consume(here, row, part):
        rows = slice(row, row + ROWS)
        part = part + biases[here]
        before = top_ref[here, rows]
        top = jnp.maximum(before, peak_of(part))
        mixed, total = weigh(part, top, with_ones(prompt_side(half_ref, 1)))
        shrink = jnp.exp2((before - top) * FACTOR)
        top_out[here, rows] = top
        total_out[here, rows] = total + total_ref[here, rows] * shrink
        mixed_out[here, rows] = mixed + mixed_ref[here, rows] * shrink

    live_rows(lengths_ref, product, consume)


def attend_rest(
    q_ref,
    half_ref,
    far_ref,
    owner_ref,
    lengths_ref,
    offsets_ref,
    top_ref,
    total_ref,
    mixed_ref,
    out_ref,
):
    base = first_sample()
    biases = prompt_biases(1 - lax.axis_index("c"), owner_ref, offsets_ref)

    def product(here, row):
        q = q_ref[here, row : row + ROWS]
        return scores(q, prompt_side(half_ref, 0)), scores(q, cont_side(far_ref, 0, here, row))

    def consume(here, row, parts):
        rows = slice(row, row + ROWS)
        length = lengths_ref[base + here]
        part = parts[0] + biases[here]
        cont = cont_mask(parts[1], True, row, length)
        before = top_ref[here, rows]
        top = jnp.maximum(before, jnp.maximum(peak_of(part), peak_of(cont)))
        mixed, total = weigh(part, top, with_ones(prompt_side(half_ref, 1)))
        more = weigh(cont, top, with_ones(cont_side(far_ref, 1, here, row)))
        shrink = jnp.exp2((before - top) * FACTOR)
        mixed += more[0] + mixed_ref[here, rows] * shrink
        total += more[1] + total_ref[here, rows] * shrink
        t = row + lax.broadcasted_iota(jnp.int32, (ROWS, 1), 0)
        out_ref[here, rows] = jnp.where(t < length, mixed / total, 0.0).astype(jnp.bfloat16)

    def blank(here, row):
        out_ref[here, row : row + ROWS] = jnp.zeros((ROWS, HEAD_SIZE), jnp.bfloat16)

    live_rows(lengths_ref, product, consume, blank)


def call(kernel, out_shape, flops, *operands):
    vmem = pl.BlockSpec(memory_space=pltpu.VMEM)
    smem = pl.BlockSpec(memory_space=pltpu.SMEM)
    return pl.pallas_call(
        kernel,
        out_shape=out_shape,
        in_specs=[smem if operand.ndim == 1 else vmem for operand in operands],
        out_specs=jax.tree.map(lambda _: vmem, out_shape),
        compiler_params=pltpu.CompilerParams(vmem_limit_bytes=24 << 20),
        cost_estimate=pl.CostEstimate(
            flops=flops, transcendentals=flops // 512, bytes_accessed=2000000
        ),
    )(*operands)


def local(queries, prompt, cont, page_owner, cont_lengths, branch_offsets):
    owner = page_owner.reshape(8, 2, 128)
    pieces = call(
        split_heads, jax.ShapeDtypeStruct((8, 2, 2, 2, 8, HEAD_SIZE), cont.dtype), 0, cont
    ).reshape(16, 2, 2, 8, HEAD_SIZE)
    mine = lax.all_to_all(pieces, ("zl", "c"), 0, 0, tiled=True)
    pair = lax.all_gather(prompt, "c")
    pair = lax.ppermute(pair, AXES, block_moves())
    spread = call(
        repeat_blocks, jax.ShapeDtypeStruct((4, 4) + pair.shape, pair.dtype), 0, pair
    )
    own = lax.all_to_all(
        spread.reshape((16,) + pair.shape), ("x", "y"), 0, 0, tiled=True
    ).reshape(spread.shape)
    beside = lax.ppermute(mine, "y", [(0, 3), (3, 0), (1, 2), (2, 1)])
    near = jnp.stack([mine, beside]).transpose(2, 3, 0, 1, 4, 5)
    near = near.reshape(2, 2, 2, 128, HEAD_SIZE)
    far = lax.ppermute(near, "y", [(0, 1), (1, 0), (2, 3), (3, 2)])
    other = lax.ppermute(own, "c", [(0, 1), (1, 0)])
    wide = jax.ShapeDtypeStruct(queries.shape, jnp.float32)
    state = call(
        attend_near,
        (wide, wide, wide),
        100000000,
        queries,
        near,
        cont_lengths,
        branch_offsets,
        owner,
    )
    state = call(
        attend_own,
        (wide, wide, wide),
        550000000,
        queries,
        own,
        owner,
        cont_lengths,
        branch_offsets,
        *state,
    )
    return call(
        attend_rest,
        jax.ShapeDtypeStruct(queries.shape, jnp.bfloat16),
        650000000,
        queries,
        other,
        far,
        owner,
        cont_lengths,
        branch_offsets,
        *state,
    )


def solution(mesh):
    fine = Mesh(mesh.devices.reshape(DIMS), AXES)
    sample, ctx = ("x", "zh"), ("zl", "y", "c")
    in_specs = (
        P(sample, None, ctx),
        P(None, ctx, sample),
        P(None, sample, ctx, None),
        P(),
        P(),
        P(),
    )
    return jax.shard_map(
        local, mesh=fine, in_specs=in_specs, out_specs=P(sample, None, ctx), check_vma=False
    )
```

```python
import jax
import jax.numpy as jnp
from jax import lax
from jax.experimental import pallas as pl
from jax.experimental.pallas import tpu as pltpu
from jax.sharding import Mesh, PartitionSpec as P


HEAD_SIZE = 128
KEY_VALUE_HEADS = 8
AXES = ("x", "zh", "zl", "y", "c")
DIMS = (4, 2, 8, 4, 2)
NEG = -1e30
FACTOR = HEAD_SIZE**-0.5 * 1.4426950408889634
ROWS = 128
TRANSPOSED = (((1,), (1,)), ((), ()))


def flat(x, zh, zl, y, c):
    return (((x * 2 + zh) * 8 + zl) * 4 + y) * 2 + c


def hops(source, target, size):
    apart = abs(source - target) % size
    return min(apart, size - apart)


def block_plan():
    plan, chunks = {}, []
    for z in range(2):
        for head in range(8):
            places = [(x, c) for x in range(4) for c in range(2)]
            places.sort(key=lambda place: hops(head // 2, place[0], 4))
            blocks = sorted(range(8), key=lambda a: -hops(8 * (head % 2) + a, head + 8 * z, 16))
            packed = 0
            for a, (x, c) in zip(blocks, places):
                plan[z, head, a] = (x, c)
                packed |= a << (12 * c + 3 * x)
            chunks.append(packed)
    return plan, chunks


PLAN, CHUNKS = block_plan()


def block_moves():
    moves = []
    for (z, head, a), (x, c) in PLAN.items():
        for y in range(4):
            moves.append((flat(head // 2, head % 2, a, y, z), flat(x, z, head, y, c)))
    return moves


def first_sample():
    return (lax.axis_index("x") * 2 + lax.axis_index("zh")) * 2


def with_ones(values):
    return jnp.concatenate([values, jnp.ones_like(values)], axis=1)


def weigh(part, top, values):
    wide = jnp.concatenate([top] * (part.shape[1] // HEAD_SIZE), axis=1)
    weights = jnp.exp2((part - wide) * FACTOR).astype(jnp.bfloat16)
    both = jnp.dot(weights, values, preferred_element_type=jnp.float32)
    return both[:, :HEAD_SIZE], both[:, HEAD_SIZE:]


def peak_of(part):
    return jnp.broadcast_to(part.max(axis=1, keepdims=True), (ROWS, HEAD_SIZE))


def split_heads(cont_ref, out_ref):
    for head in range(KEY_VALUE_HEADS):
        piece = cont_ref[:, :, :, head * HEAD_SIZE : (head + 1) * HEAD_SIZE]
        for core in range(2):
            out_ref[head, core] = piece


def repeat_blocks(pair_ref, out_ref):
    pair = pair_ref[...]
    for x in range(4):
        for y in range(4):
            out_ref[x, y] = pair


def run_tiles(tiles, product, consume):
    ahead = product(*tiles[0])
    for index, tile in enumerate(tiles):
        part = ahead
        if index + 1 < len(tiles):
            ahead = product(*tiles[index + 1])
        consume(*tile, part)


def live_rows(lengths_ref, product, consume, blank=None, ready=None):
    base = first_sample()
    run_tiles([(here, row) for here in range(2) for row in (0, ROWS)], product, consume)
    if ready is not None:
        for here in range(2):
            ready(here, 0)
    for here in range(2):
        length = lengths_ref[base + here]
        tiles = [(here, 2 * ROWS), (here, 3 * ROWS)]

        @pl.when(length > 3 * ROWS)
        def _():
            run_tiles(tiles, product, consume)

        @pl.when((length > 2 * ROWS) & (length <= 3 * ROWS))
        def _():
            run_tiles(tiles[:1], product, consume)
            if blank is not None:
                blank(*tiles[1])

        if blank is not None:

            @pl.when(length <= 2 * ROWS)
            def _():
                for tile in tiles:
                    blank(*tile)

        if ready is not None:
            ready(here, 2 * ROWS)


def prompt_side(half_ref, kind):
    return half_ref[:, :, :, kind].reshape(1024, HEAD_SIZE)


def prompt_biases(which, owner_ref, offsets_ref):
    base = first_sample()
    plane = lax.axis_index("zh") * 8 + lax.axis_index("zl")
    packed = jnp.int32(0)
    for index, chunks in enumerate(CHUNKS):
        packed = jnp.where(plane == index, jnp.int32(chunks), packed)
    col = lax.broadcasted_iota(jnp.int32, (1, 256), 1)
    owners, places = [], []
    for x in range(4):
        chunk = (packed >> (12 * which + 3 * x)) & 7
        owner = owner_ref[chunk]
        owners += [owner[0:1], owner[1:2]]
        places.append(chunk * 256 + col)
    owner = jnp.concatenate(owners, axis=1)
    place = jnp.concatenate(places, axis=1)
    biases = []
    for here in range(2):
        seen = (owner == 0) | (owner == base + here + 1)
        biases.append(jnp.where(seen & (place < offsets_ref[base + here]), 0.0, NEG))
    return biases


def scores(q, keys):
    return lax.dot_general(q, keys, TRANSPOSED, preferred_element_type=jnp.float32)


def cont_side(ref, kind, here, row):
    count = 64 if row < 2 * ROWS else 128
    return jnp.concatenate([ref[kind, here, 0, :count], ref[kind, here, 1, :count]])


def cont_mask(cont, far, row, length):
    count = cont.shape[1] // 2
    col = lax.broadcasted_iota(jnp.int32, (1, 2 * count), 1)
    step = (col >= count).astype(jnp.int32)
    col = col - step * count
    y = lax.axis_index("y") ^ (3 * step) ^ (1 if far else 0)
    u = (col >> 4) * 64 + y * 16 + (col & 15)
    t = row + lax.broadcasted_iota(jnp.int32, (ROWS, 1), 0)
    return jnp.where(u <= jnp.minimum(t, length - 1), cont, NEG)


def attend_near(
    q_ref, near_ref, lengths_ref, offsets_ref, owner_ref, top_ref, total_ref, mixed_ref
):
    base = first_sample()

    def product(here, row):
        return scores(q_ref[here, row : row + ROWS], cont_side(near_ref, 0, here, row))

    def consume(here, row, cont):
        cont = cont_mask(cont, False, row, lengths_ref[base + here])
        top = peak_of(cont)
        mixed, total = weigh(cont, top, with_ones(cont_side(near_ref, 1, here, row)))
        top_ref[here, row : row + ROWS] = top
        total_ref[here, row : row + ROWS] = total
        mixed_ref[here, row : row + ROWS] = mixed

    live_rows(lengths_ref, product, consume)


def attend_own(
    q_ref,
    half_ref,
    owner_ref,
    lengths_ref,
    offsets_ref,
    top_ref,
    total_ref,
    mixed_ref,
    top_out,
    total_out,
    mixed_out,
):
    biases = prompt_biases(lax.axis_index("c"), owner_ref, offsets_ref)

    def product(here, row):
        return scores(q_ref[here, row : row + ROWS], prompt_side(half_ref, 0))

    def consume(here, row, part):
        rows = slice(row, row + ROWS)
        part = part + biases[here]
        before = top_ref[here, rows]
        top = jnp.maximum(before, peak_of(part))
        mixed, total = weigh(part, top, with_ones(prompt_side(half_ref, 1)))
        shrink = jnp.exp2((before - top) * FACTOR)
        top_out[here, rows] = top
        total_out[here, rows] = total + total_ref[here, rows] * shrink
        mixed_out[here, rows] = mixed + mixed_ref[here, rows] * shrink

    live_rows(lengths_ref, product, consume)


def attend_rest(
    q_ref,
    half_ref,
    far_ref,
    owner_ref,
    lengths_ref,
    offsets_ref,
    top_ref,
    total_ref,
    mixed_ref,
    out_ref,
    held,
    sent,
):
    base = first_sample()
    biases = prompt_biases(1 - lax.axis_index("c"), owner_ref, offsets_ref)

    def product(here, row):
        q = q_ref[here, row : row + ROWS]
        return scores(q, prompt_side(half_ref, 0)), scores(q, cont_side(far_ref, 0, here, row))

    def consume(here, row, parts):
        rows = slice(row, row + ROWS)
        length = lengths_ref[base + here]
        part = parts[0] + biases[here]
        cont = cont_mask(parts[1], True, row, length)
        before = top_ref[here, rows]
        top = jnp.maximum(before, jnp.maximum(peak_of(part), peak_of(cont)))
        mixed, total = weigh(part, top, with_ones(prompt_side(half_ref, 1)))
        more = weigh(cont, top, with_ones(cont_side(far_ref, 1, here, row)))
        shrink = jnp.exp2((before - top) * FACTOR)
        mixed += more[0] + mixed_ref[here, rows] * shrink
        total += more[1] + total_ref[here, rows] * shrink
        t = row + lax.broadcasted_iota(jnp.int32, (ROWS, 1), 0)
        held[here, rows] = jnp.where(t < length, mixed / total, 0.0).astype(jnp.bfloat16)

    def blank(here, row):
        held[here, row : row + ROWS] = jnp.zeros((ROWS, HEAD_SIZE), jnp.bfloat16)

    copies = []

    def ready(here, row):
        rows = pl.ds(row, 2 * ROWS)
        copies.append(
            pltpu.make_async_copy(
                held.at[here, rows], out_ref.at[here, rows], sent.at[here, row // (2 * ROWS)]
            )
        )
        copies[-1].start()

    live_rows(lengths_ref, product, consume, blank, ready)
    for copy in copies:
        copy.wait()


def call(kernel, out_shape, flops, *operands, out_space=pltpu.VMEM, scratch=()):
    vmem = pl.BlockSpec(memory_space=pltpu.VMEM)
    smem = pl.BlockSpec(memory_space=pltpu.SMEM)
    return pl.pallas_call(
        kernel,
        out_shape=out_shape,
        in_specs=[smem if operand.ndim == 1 else vmem for operand in operands],
        out_specs=jax.tree.map(lambda _: pl.BlockSpec(memory_space=out_space), out_shape),
        scratch_shapes=scratch,
        compiler_params=pltpu.CompilerParams(vmem_limit_bytes=24 << 20),
        cost_estimate=pl.CostEstimate(
            flops=flops, transcendentals=flops // 512, bytes_accessed=2000000
        ),
    )(*operands)


def local(queries, prompt, cont, page_owner, cont_lengths, branch_offsets):
    owner = page_owner.reshape(8, 2, 128)
    pieces = call(
        split_heads, jax.ShapeDtypeStruct((8, 2, 2, 2, 8, HEAD_SIZE), cont.dtype), 0, cont
    ).reshape(16, 2, 2, 8, HEAD_SIZE)
    mine = lax.all_to_all(pieces, ("zl", "c"), 0, 0, tiled=True)
    pair = lax.all_gather(prompt, "c")
    pair = lax.ppermute(pair, AXES, block_moves())
    spread = call(repeat_blocks, jax.ShapeDtypeStruct((4, 4) + pair.shape, pair.dtype), 0, pair)
    own = lax.all_to_all(
        spread.reshape((16,) + pair.shape), ("x", "y"), 0, 0, tiled=True
    ).reshape(spread.shape)
    beside = lax.ppermute(mine, "y", [(0, 3), (3, 0), (1, 2), (2, 1)])
    near = jnp.stack([mine, beside]).transpose(2, 3, 0, 1, 4, 5)
    near = near.reshape(2, 2, 2, 128, HEAD_SIZE)
    far = lax.ppermute(near, "y", [(0, 1), (1, 0), (2, 3), (3, 2)])
    other = lax.ppermute(own, "c", [(0, 1), (1, 0)])
    wide = jax.ShapeDtypeStruct(queries.shape, jnp.float32)
    state = call(
        attend_near,
        (wide, wide, wide),
        100000000,
        queries,
        near,
        cont_lengths,
        branch_offsets,
        owner,
    )
    state = call(
        attend_own,
        (wide, wide, wide),
        550000000,
        queries,
        own,
        owner,
        cont_lengths,
        branch_offsets,
        *state,
    )
    return call(
        attend_rest,
        jax.ShapeDtypeStruct(queries.shape, jnp.bfloat16),
        650000000,
        queries,
        other,
        far,
        owner,
        cont_lengths,
        branch_offsets,
        *state,
        out_space=pltpu.HBM,
        scratch=[
            pltpu.VMEM(queries.shape, jnp.bfloat16),
            pltpu.SemaphoreType.DMA((2, 2)),
        ],
    )


def solution(mesh):
    fine = Mesh(mesh.devices.reshape(DIMS), AXES)
    sample, ctx = ("x", "zh"), ("zl", "y", "c")
    in_specs = (
        P(sample, None, ctx),
        P(None, ctx, sample),
        P(None, sample, ctx, None),
        P(),
        P(),
        P(),
    )
    return jax.shard_map(
        local, mesh=fine, in_specs=in_specs, out_specs=P(sample, None, ctx), check_vma=False
    )
```
